256 devices in a mesh: grp: 8 (over y_lo, x), sx: 4 (over y_hi, core), sz: 8 (over z).
Axes of the slice: x: 4, y: 4 (y_hi: 2, y_lo: 2; y = y_hi * 2 + y_lo), z: 8, core: 2. Of those that a mesh axis runs over, the one named last changes fastest.
Arguments:
- radiant_density_before: float32 [16, 64, 128, 1024], P('grp', 'sx', None, 'sz'), may hold values from 0.2 to 6, as said below
- grain_kelvin_before: float32 [64, 128, 1024], P('sx', None, 'sz'), may hold values from 0.5 to 1.5
- grain_thermal_capacity: float32 [64, 128, 1024], P('sx', None, 'sz'), may hold values from 0.3 to 3
- grain_species_index: int32 [64, 128, 1024], P('sx', None, 'sz'), may hold values from 0 to 7
- band_absorptivity_table: float32 [8, 16], P(None, 'grp'), may hold values from 0.2 to 5
- blackbody_band_fraction: float32 [16], P('grp'), may hold values from 0.05 to 0.5
Outputs:
- radiant_density_after: float32 [16, 64, 128, 1024], P('grp', 'sx', None, 'sz')
- grain_kelvin_after: float32 [64, 128, 1024], P('sx', None, 'sz')
The draws below stay inside these ranges and needn't reach their ends.
Inputs may be any that keep to these rules, and one draw needn't show every extreme that they name: `radiant_density_before`: positive everywhere.
All inputs are finite; a program needn't handle non-finite values.
Results may differ from the reference program's by a relative error of at most 0.0003.
Values sent between devices are 32-bit elements; how exact they have to be, the bound alone decides.
No kernel may reach another device: no remote copies, remote signals or barrier semaphores. Data moves between devices by JAX's collectives and lax.ppermute only.
A program may use at most 128 MiB of HBM per device.

```python
import math
import jax
import jax.numpy as jnp
from jax import lax

G = 16
MAT = 8
ITERS = 3
MESH_SPAN_EAST = 64
MESH_SPAN_NORTH = 128
MESH_SPAN_UPWARD = 1024


def draw_radiant_density_before(key, part):
    key_base = jax.random.fold_in(key, 11)
    xpos = jnp.arange(MESH_SPAN_EAST, dtype=jnp.float32) / max(MESH_SPAN_EAST - 1, 1)
    zpos = jnp.arange(MESH_SPAN_UPWARD, dtype=jnp.float32) / max(MESH_SPAN_UPWARD - 1, 1)
    ramp = 1.0 + xpos[:, None, None] + zpos[None, None, :]
    logs = jax.random.uniform(key_base, (G, MESH_SPAN_EAST, MESH_SPAN_NORTH, MESH_SPAN_UPWARD), jnp.float32, jnp.log(0.2), jnp.log(2.0))
    base = jnp.exp(logs)
    return (base * ramp[None]).astype(jnp.float32)


def set_ends(array, rng, least, high):
    index_at = [jax.random.randint(jax.random.fold_in(rng, axis), (), 0, length) for axis, length in enumerate(array.shape)]
    main_axis = array.shape.index(max(array.shape))
    neighbour = index_at[:main_axis] + [(index_at[main_axis] + 1) % array.shape[main_axis]] + index_at[main_axis + 1:]
    return array.at[tuple(index_at)].set(least).at[tuple(neighbour)].set(high)


def steps_of(stream_key, dims, pieces, least, high):
    def one(dim, blocks):
        heights = jax.random.uniform(jax.random.fold_in(jax.random.fold_in(stream_key, 6), dim), (blocks,), jnp.float32, least / len(pieces), high / len(pieces))
        return jnp.repeat(jnp.exp(heights), dims[dim] // blocks).reshape((-1,) + (1,) * (len(dims) - dim - 1))

    factor_of = one(*pieces[0])
    for cut in pieces[1:]:
        factor_of = factor_of * one(*cut)
    return factor_of


def setup_inputs(seed: int = 0) -> dict:
    streams_of = jax.random.split(jax.random.key(seed), 7)
    return {
        "radiant_density_before": draw_radiant_density_before(jax.random.fold_in(streams_of[6], 71), 0),
        "grain_kelvin_before": jnp.clip(jnp.exp(math.log(1.5) - 1.0986123 * jax.random.uniform(streams_of[1], (MESH_SPAN_EAST, MESH_SPAN_NORTH, MESH_SPAN_UPWARD), jnp.float32) ** steps_of(streams_of[1], (MESH_SPAN_EAST, MESH_SPAN_NORTH, MESH_SPAN_UPWARD), ((0, 4), (2, 8)), -0.2, 0.2)), 0.5, 1.5),
        "grain_thermal_capacity": jnp.clip(jnp.exp(math.log(3.0) - 2.3025851 * jax.random.uniform(streams_of[2], (MESH_SPAN_EAST, MESH_SPAN_NORTH, MESH_SPAN_UPWARD), jnp.float32) ** steps_of(streams_of[2], (MESH_SPAN_EAST, MESH_SPAN_NORTH, MESH_SPAN_UPWARD), ((0, 4), (2, 8)), -0.2, 0.2)), 0.3, 3.0),
        "grain_species_index": set_ends(jax.random.randint(streams_of[3], (MESH_SPAN_EAST, MESH_SPAN_NORTH, MESH_SPAN_UPWARD), 0, MAT), jax.random.fold_in(streams_of[3], 1), 0, MAT - 1).astype(jnp.int32),
        "band_absorptivity_table": jnp.clip(jnp.exp(math.log(5.0) - 3.218876 * jax.random.uniform(streams_of[4], (MAT, G), jnp.float32) ** steps_of(streams_of[4], (MAT, G), ((1, 8),), -0.2, 0.2)), 0.2, 5.0),
        "blackbody_band_fraction": jnp.clip(jnp.exp(math.log(0.5) - 2.3025851 * jax.random.uniform(streams_of[5], (G,), jnp.float32) ** steps_of(streams_of[5], (G,), ((0, 8),), -0.2, 0.2)), 0.05, 0.5),
    }


interval_length_seconds = 0.5

def coefficient(extended, opacity, center):
    grad_x = (extended[..., 2:, 1:-1, 1:-1] - extended[..., :-2, 1:-1, 1:-1]) * 0.5
    grad_y = (extended[..., 1:-1, 2:, 1:-1] - extended[..., 1:-1, :-2, 1:-1]) * 0.5
    grad_z = (extended[..., 1:-1, 1:-1, 2:] - extended[..., 1:-1, 1:-1, :-2]) * 0.5
    ratio = jnp.sqrt(grad_x * grad_x + grad_y * grad_y + grad_z * grad_z) / (opacity * center)
    limiter = (2.0 + ratio) / (6.0 + 3.0 * ratio + ratio * ratio)
    return limiter / opacity

def stencil(padded, absorption, diff_ext):
    center = padded[..., 1:-1, 1:-1, 1:-1]
    diff_mid = diff_ext[..., 1:-1, 1:-1, 1:-1]
    total = absorption * center
    shifts = [(slice(2, None), slice(1, -1), slice(1, -1)), (slice(None, -2), slice(1, -1), slice(1, -1)), (slice(1, -1), slice(2, None), slice(1, -1)), (slice(1, -1), slice(None, -2), slice(1, -1)), (slice(1, -1), slice(1, -1), slice(2, None)), (slice(1, -1), slice(1, -1), slice(None, -2))]
    for sel in shifts:
        index_tuple = (...,) + sel
        total = total + 0.5 * (diff_mid + diff_ext[index_tuple]) * (center - padded[index_tuple])
    return total

def reference(radiant_density_before, grain_kelvin_before, grain_thermal_capacity, grain_species_index, band_absorptivity_table, blackbody_band_fraction):
    thermal_fourth_moment = grain_kelvin_before ** 4
    thermal_third_moment = grain_kelvin_before ** 3

    def accumulate(carry, items):
        field, table_col, weight = items
        opacity = table_col[grain_species_index]
        combined_absorbed_rate = carry[0] + opacity * (field - weight * thermal_fourth_moment)
        combined_derivative_rate = carry[1] + 4.0 * opacity * weight * thermal_third_moment
        return ((combined_absorbed_rate, combined_derivative_rate), None)
    blank_array_holder = jnp.zeros(grain_kelvin_before.shape, jnp.float32)
    (combined_absorbed_rate, combined_derivative_rate), _ = lax.scan(accumulate, (blank_array_holder, blank_array_holder), (radiant_density_before, band_absorptivity_table.T, blackbody_band_fraction))
    grain_kelvin_after = grain_kelvin_before + interval_length_seconds * combined_absorbed_rate / (grain_thermal_capacity + interval_length_seconds * combined_derivative_rate)
    blackbody_fourth_order = grain_kelvin_after ** 4

    def solve(items):
        field, table_col, weight = items
        opacity = table_col[grain_species_index]
        source = field / interval_length_seconds + opacity * weight * blackbody_fourth_order
        diffusion = coefficient(jnp.pad(field, 1), opacity, field)
        diff_ext = jnp.pad(diffusion, 1)
        absorption = 1.0 / interval_length_seconds + opacity

        def operate(vector):
            return stencil(jnp.pad(vector, 1), absorption, diff_ext)
        radiant_density_answer = field
        residual = source - operate(radiant_density_answer)
        direction = residual
        norm_now = jnp.sum(residual * residual)
        for step in range(ITERS):
            image = operate(direction)
            alpha = norm_now / jnp.sum(direction * image)
            radiant_density_answer = radiant_density_answer + alpha * direction
            residual = residual - alpha * image
            if step + 1 < ITERS:
                norm_next = jnp.sum(residual * residual)
                direction = residual + norm_next / norm_now * direction
                norm_now = norm_next
        return radiant_density_answer
    radiant_density_after = lax.map(solve, (radiant_density_before, band_absorptivity_table.T, blackbody_band_fraction))
    return (radiant_density_after, grain_kelvin_after)
```

```python
import functools

import jax
import jax.numpy as jnp
from jax import lax
from jax.experimental import pallas as pl
from jax.experimental.pallas import tpu as pltpu
from jax.sharding import PartitionSpec as P

DT = 0.5
SHIFT = 6.0
SCALE = 4.0
NX = 16
N = 128
MATS = 8
HE = 5
HT = 3
ROWS = 152
ZO = 12
RC = 8
NC = 136
PX = 24
CHUNKS = ((8, 48), (56, 48), (104, 40))
OWN = ((12, 48), (60, 48), (108, 32))

SX_A = [(0, 1), (1, 0), (2, 3), (3, 2)]
SX_B = [(1, 2), (2, 1), (3, 0), (0, 3)]
SZ_A = [(0, 1), (1, 0), (2, 3), (3, 2), (4, 5), (5, 4), (6, 7), (7, 6)]
SZ_B = [(1, 2), (2, 1), (3, 4), (4, 3), (5, 6), (6, 5), (7, 0), (0, 7)]

VM = pl.BlockSpec(memory_space=pltpu.VMEM)
SM = pl.BlockSpec(memory_space=pltpu.SMEM)
F32 = jnp.float32


def shaped(*dims):
    return jax.ShapeDtypeStruct(dims, F32)


def params(mib):
    return pltpu.CompilerParams(vmem_limit_bytes=mib * 1024 * 1024)


def cost(flops, nbytes):
    return pl.CostEstimate(flops=flops, bytes_accessed=nbytes, transcendentals=0)


def pick(species, values):
    b0, b1, b2 = ((species & k) != 0 for k in (1, 2, 4))
    level = [jnp.where(b0, values[2 * k + 1], values[2 * k]) for k in range(4)]
    level = [jnp.where(b1, level[1], level[0]), jnp.where(b1, level[3], level[2])]
    return jnp.where(b2, level[1], level[0])


def absorbed_kernel(e_ref, sp_ref, tab_ref, w_ref, out_ref):
    i = pl.program_id(0)
    tabs = [[tab_ref[m, g] for m in range(MATS)] for g in range(2)]

    @pl.when(i == 0)
    def _():
        for m in range(MATS):
            share = tabs[0][m] * w_ref[0] + tabs[1][m] * w_ref[1]
            for k in range(8):
                out_ref[k, NX, m : m + 1, :] = jnp.full((1, N), share, F32)
        for k in range(8):
            out_ref[k, NX, 8:16, :] = jnp.zeros((8, N), F32)

    for x in range(4):
        for k in range(4):
            rows = slice(k * 32, k * 32 + 32)
            species = sp_ref[x, rows, :]
            total = pick(species, tabs[0]) * e_ref[0, x, rows, :] + pick(species, tabs[1]) * e_ref[1, x, rows, :]
            out_ref[2 * k, i * 4 + x] = total[:16]
            out_ref[2 * k + 1, i * 4 + x] = total[16:]


def turn_kernel(e_ref, sp_ref, out_ref, a_ref, b_ref):
    i = pl.program_id(0)
    for x in range(2):
        for g in range(2):
            out_ref[g, i * 2 + x] = e_ref[g, x].T
        out_ref[2, i * 2 + x] = sp_ref[x].astype(F32).T

    @pl.when(i == pl.num_programs(0) - 1)
    def _():
        even = lax.rem(lax.axis_index("sx"), 2) == 0
        to_a = jnp.where(even, NX - HE, 0)
        to_b = jnp.where(even, 0, NX - HE)
        for c in range(3):
            for j in range(HE):
                a_ref[c, j] = out_ref[c, to_a + j]
                b_ref[c, j] = out_ref[c, to_b + j]


def edge_rows(get, depth, a_ref, b_ref):
    even = lax.rem(lax.axis_index("sz"), 2) == 0
    to_a = pl.multiple_of(jnp.where(even, N - 8, 0), 8)
    to_b = pl.multiple_of(jnp.where(even, 0, N - 8), 8)
    for x in range(depth):
        a_ref[x] = get(x, to_a)
        b_ref[x] = get(x, to_b)


def corner_kernel(c_count, halo, own_ref, xa_ref, xb_ref, a_ref, b_ref):
    even = lax.rem(lax.axis_index("sx"), 2) == 0
    for c in range(c_count):

        def fill(low, high):
            def get(x, row):
                if x < halo:
                    return low[c, x, pl.ds(row, 8), :]
                if x < halo + NX:
                    return own_ref[c, x - halo, pl.ds(row, 8), :]
                return high[c, x - halo - NX, pl.ds(row, 8), :]

            edge_rows(get, NX + 2 * halo, a_ref.at[c], b_ref.at[c])

        pl.when(even)(lambda: fill(xb_ref, xa_ref))
        pl.when(jnp.logical_not(even))(lambda: fill(xa_ref, xb_ref))


def assemble(c, halo, own_ref, xa_ref, xb_ref, za_ref, zb_ref, put):
    x_even = lax.rem(lax.axis_index("sx"), 2) == 0
    z_even = lax.rem(lax.axis_index("sz"), 2) == 0

    def copy(first, ref, offset, count, row):
        def step(j, carry):
            put(first + j, row, ref[c, offset + j])
            return carry

        lax.fori_loop(0, count, step, 0)

    copy(halo, own_ref, 0, NX, ZO)

    @pl.when(x_even)
    def _():
        copy(0, xb_ref, 0, halo, ZO)
        copy(halo + NX, xa_ref, 0, halo, ZO)

    @pl.when(jnp.logical_not(x_even))
    def _():
        copy(0, xa_ref, 0, halo, ZO)
        copy(halo + NX, xb_ref, 0, halo, ZO)

    @pl.when(z_even)
    def _():
        copy(0, zb_ref, 0, NX + 2 * halo, ZO - 8)
        copy(0, za_ref, 0, NX + 2 * halo, ZO + N)

    @pl.when(jnp.logical_not(z_even))
    def _():
        copy(0, za_ref, 0, NX + 2 * halo, ZO - 8)
        copy(0, zb_ref, 0, NX + 2 * halo, ZO + N)


def matrix_kernel(
    own_ref, xa_ref, xb_ref, za_ref, zb_ref, tab_ref, w_ref,
    dg_ref, kx_ref, ky_ref, kz_ref, q_ref, ow_ref,
    e_ref, sp_ref, d_ref, op_ref,
):
    sx, sz = lax.axis_index("sx"), lax.axis_index("sz")
    tabs = [[tab_ref[m, g] for m in range(MATS)] for g in range(2)]

    def put_e(g):
        def put(x, row, value):
            e_ref[g, x, row : row + value.shape[0], :] = value

        return put

    def put_s(x, row, value):
        sp_ref[x, row : row + value.shape[0], :] = value

    for c in range(3):
        assemble(c, HE, own_ref, xa_ref, xb_ref, za_ref, zb_ref, put_s if c == 2 else put_e(c))

    def clear_planes(first):
        def step(j, carry):
            for g in range(2):
                e_ref[g, first + j] = jnp.zeros((ROWS, N), F32)
            return carry

        lax.fori_loop(0, HE, step, 0)

    def clear_rows(row):
        def step(j, carry):
            for g in range(2):
                e_ref[g, j, row : row + 8, :] = jnp.zeros((8, N), F32)
            return carry

        lax.fori_loop(0, NX + 2 * HE, step, 0)

    pl.when(sx == 0)(lambda: clear_planes(0))
    pl.when(sx == 3)(lambda: clear_planes(HE + NX))
    pl.when(sz == 0)(lambda: clear_rows(ZO - 8))
    pl.when(sz == 7)(lambda: clear_rows(ZO + N))

    def lanes(n):
        return lax.broadcasted_iota(jnp.int32, (n, N), 1)

    def height(row, n):
        return lax.broadcasted_iota(jnp.int32, (n, N), 0) + (sz * N + row - ZO)

    def coefficients(p, carry):
        gx = sx * NX + p - 4
        x_in = jnp.logical_and(gx >= 0, gx < 4 * NX).astype(jnp.int32)
        for row, n in CHUNKS:
            gz = height(row, n)
            inside = jnp.logical_and(gz >= 0, gz < 8 * N * x_in)
            lane = lanes(n)
            rows = slice(row, row + n)
            species = sp_ref[p + 1, rows, :].astype(jnp.int32)
            for g in range(2):
                opacity = pick(species, tabs[g])
                center = e_ref[g, p + 1, rows, :]
                dx = e_ref[g, p + 2, rows, :] - e_ref[g, p, rows, :]
                dz = e_ref[g, p + 1, row + 1 : row + 1 + n, :] - e_ref[g, p + 1, row - 1 : row - 1 + n, :]
                above = jnp.where(lane == N - 1, 0.0, pltpu.roll(center, N - 1, 1))
                below = jnp.where(lane == 0, 0.0, pltpu.roll(center, 1, 1))
                dy = above - below
                square = 0.25 * (dx * dx + dy * dy + dz * dz)
                slope = jnp.sqrt(square)
                m = opacity * center
                upper = m * (2.0 * m + slope)
                lower = opacity * (m * (6.0 * m + 3.0 * slope) + square)
                d_ref[g, p, rows, :] = jnp.where(inside, upper / lower, 0.0)
                op_ref[g, p, rows, :] = opacity
        return carry

    lax.fori_loop(0, PX, coefficients, 0)

    inv = 1.0 / SCALE

    def operator(p, carry):
        gx = sx * NX + p - 4
        x_in = jnp.logical_and(gx >= 0, gx < 4 * NX).astype(jnp.int32)
        x_face = jnp.where(jnp.logical_and(gx >= 0, gx + 1 < 4 * NX), 0.5, 0.0)
        for row, n in CHUNKS:
            gz = height(row, n)
            inside = jnp.logical_and(gz >= 0, gz < 8 * N * x_in)
            z_face = jnp.where(jnp.logical_and(gz >= 0, gz + 1 < 8 * N), 0.5, 0.0)
            lane = lanes(n)
            rows = slice(row, row + n)
            up = slice(row + 1, row + 1 + n)
            down = slice(row - 1, row - 1 + n)
            for g in range(2):
                d = d_ref[g, p, rows, :]
                dxp, dxm = d_ref[g, p + 1, rows, :], d_ref[g, p - 1, rows, :]
                dzp, dzm = d_ref[g, p, up, :], d_ref[g, p, down, :]
                dyp = jnp.where(lane == N - 1, 0.0, pltpu.roll(d, N - 1, 1))
                dym = jnp.where(lane == 0, 0.0, pltpu.roll(d, 1, 1))
                opacity = op_ref[g, p, rows, :]
                sxp, sxm, szp, szm, syp, sym = (d + o for o in (dxp, dxm, dzp, dzm, dyp, dym))
                total = 0.5 * (((sxp + sxm) + (szp + szm)) + (syp + sym))
                diag = (1.0 / DT + opacity) + total
                center = e_ref[g, p + 1, rows, :]
                moved = (
                    (sxp * e_ref[g, p + 2, rows, :] + sxm * e_ref[g, p, rows, :])
                    + (szp * e_ref[g, p + 1, up, :] + szm * e_ref[g, p + 1, down, :])
                    + jnp.where(lane == N - 1, 0.0, syp * pltpu.roll(center, N - 1, 1))
                    + jnp.where(lane == 0, 0.0, sym * pltpu.roll(center, 1, 1))
                )
                q_ref[g, p, rows, :] = jnp.where(inside, (1.0 / DT - diag) * center + 0.5 * moved, 0.0)
                ow_ref[g, p, rows, :] = jnp.where(inside, opacity * w_ref[g], 0.0)
                dg_ref[g, p, rows, :] = jnp.where(inside, (diag - SHIFT) * inv, 0.0)
                kx_ref[g, p, rows, :] = sxp * (x_face * inv)
                kz_ref[g, p, rows, :] = szp * (z_face * inv)
                ky_ref[g, p, rows, :] = jnp.where(lane == N - 1, 0.0, syp * (0.5 * inv))
        return carry

    lax.fori_loop(1, PX - 1, operator, 0)


def temperature_kernel(g_ref, r_ref, t_ref, cap_ref, sp_ref, out_ref):
    shares = r_ref[0, NX, 0:8, :]
    for k in range(1, 8):
        shares = shares + r_ref[k, NX, 0:8, :]
    values = [jnp.broadcast_to(shares[m : m + 1, :], (16, N)) for m in range(MATS)]
    for x in range(NX):
        absorbed = r_ref[0, x]
        for k in range(1, 8):
            absorbed = absorbed + r_ref[k, x]
        t = t_ref[x]
        weight = pick(sp_ref[x], values)
        cube = t * t * t
        gain = absorbed - weight * (cube * t)
        slope = 4.0 * weight * cube
        after = t + DT * gain / (cap_ref[x] + DT * slope)
        for k in range(8):
            out_ref[k, x] = after


def emission_kernel(t_ref, out_ref, a_ref, b_ref):
    for x in range(NX):
        t = t_ref[:, x].reshape(N, N)
        square = t * t
        out_ref[0, x] = (square * square).T
    even = lax.rem(lax.axis_index("sx"), 2) == 0
    to_a = jnp.where(even, NX - HT, 0)
    to_b = jnp.where(even, 0, NX - HT)
    for j in range(HT):
        a_ref[0, j] = out_ref[0, to_a + j]
        b_ref[0, j] = out_ref[0, to_b + j]


def krylov_kernel(
    own_ref, xa_ref, xb_ref, za_ref, zb_ref, dg_ref, kx_ref, ky_ref, kz_ref, q_ref, ow_ref,
    v0_ref, v1_ref, v2_ref, mom_ref, t_ref,
):
    def put(x, row, value):
        t_ref[x, row : row + value.shape[0], :] = value

    assemble(0, HT, own_ref, xa_ref, xb_ref, za_ref, zb_ref, put)

    def first(p, carry):
        for row, n in CHUNKS:
            rows = slice(row, row + n)
            t = t_ref[p - 1, rows, :]
            for g in range(2):
                v0_ref[g, p, rows, :] = q_ref[g, p, rows, :] + ow_ref[g, p, rows, :] * t
        return carry

    lax.fori_loop(1, PX - 1, first, 0)

    def apply(v_ref, g, p, row, n):
        rows = slice(row, row + n)
        up = slice(row + 1, row + 1 + n)
        down = slice(row - 1, row - 1 + n)
        c = v_ref[g, p, rows, :]
        ky = ky_ref[g, p, rows, :]
        total = dg_ref[g, p, rows, :] * c
        total = total - kx_ref[g, p, rows, :] * v_ref[g, p + 1, rows, :]
        total = total - kx_ref[g, p - 1, rows, :] * v_ref[g, p - 1, rows, :]
        total = total - kz_ref[g, p, rows, :] * v_ref[g, p, up, :]
        total = total - kz_ref[g, p, down, :] * v_ref[g, p, down, :]
        total = total - ky * pltpu.roll(c, N - 1, 1)
        return total - pltpu.roll(ky * c, 1, 1)

    for source, target, start in ((v0_ref, v1_ref, 2), (v1_ref, v2_ref, 3)):

        def step(p, carry, source=source, target=target):
            for g in range(2):
                for row, n in CHUNKS:
                    target[g, p, row : row + n, :] = apply(source, g, p, row, n)
            return carry

        lax.fori_loop(start, PX - start, step, 0)

    def fold(value):
        return jnp.sum(value.reshape(-1, 8, N), axis=0)

    for g in range(2):

        def last(p, sums, g=g):
            sums = list(sums)
            for row, n in OWN:
                rows = slice(row, row + n)
                a, b, c = v0_ref[g, p, rows, :], v1_ref[g, p, rows, :], v2_ref[g, p, rows, :]
                d = apply(v2_ref, g, p, row, n)
                for k, (l, r) in enumerate(((a, a), (a, b), (b, b), (b, c), (c, c), (c, d))):
                    sums[k] = sums[k] + fold(l * r)
            return tuple(sums)

        sums = lax.fori_loop(4, 4 + NX, last, (jnp.zeros((8, N), F32),) * 6)
        for k in range(6):
            line = jnp.sum(sums[k], axis=0, keepdims=True)
            for peer in range(mom_ref.shape[0]):
                mom_ref[peer, g * 8 + k : g * 8 + k + 1, :] = line
        for peer in range(mom_ref.shape[0]):
            mom_ref[peer, g * 8 + 6 : g * 8 + 8, :] = jnp.zeros((2, N), F32)


def turn_back_kernel(v0_ref, v1_ref, v2_ref, out_ref):
    for k, ref in enumerate((v0_ref, v1_ref, v2_ref)):

        def step(x, carry, k=k, ref=ref):
            for g in range(2):
                out_ref[k, g, x] = ref[g, x + 4, ZO : ZO + N, :].T
            return carry

        lax.fori_loop(0, NX, step, 0)


def update_kernel(mom_ref, e_ref, v_ref, out_ref, c_ref):
    @pl.when(pl.program_id(0) == 0)
    def _():
        total = mom_ref[0]
        for k in range(1, mom_ref.shape[0]):
            total = total + mom_ref[k]
        total = jnp.sum(total, axis=1, keepdims=True)
        for g in range(2):
            n = [total[g * 8 + k : g * 8 + k + 1, :] for k in range(6)]
            m = [SHIFT * n[k] + SCALE * n[k + 1] for k in range(5)]
            l1 = m[1] / m[0]
            l2 = m[2] / m[0]
            p1 = m[2] - l1 * m[1]
            u = m[3] - l1 * m[2]
            r1 = n[1] - l1 * n[0]
            ok1 = p1 > 1e-6 * m[2]
            s1 = jnp.where(ok1, u / p1, 0.0)
            p2 = m[4] - l2 * m[2] - s1 * u
            r2 = n[2] - l2 * n[0] - s1 * r1
            ok2 = jnp.logical_and(ok1, p2 > 1e-6 * m[4])
            c2 = jnp.where(ok2, r2 / p2, 0.0)
            c1 = jnp.where(ok1, (r1 - u * c2) / p1, 0.0)
            c0 = (n[0] - m[1] * c1 - m[2] * c2) / m[0]
            for k, c in enumerate((c0, c1, c2)):
                c_ref[g * 3 + k] = jnp.broadcast_to(c, (8, N))

    for x in range(4):
        for g in range(2):
            total = e_ref[g, x]
            for k in range(3):
                total = total + v_ref[k, g, x] * c_ref[g * 3 + k, 0:1, :]
            out_ref[g, x] = total


def exchange(a, b, axis, pair_a, pair_b):
    return lax.ppermute(a, axis, pair_a), lax.ppermute(b, axis, pair_b)


def shards(energy, kelvin, capacity, species, table, fraction):
    planes = lambda k: pl.BlockSpec((2, k, N, N), lambda i: (0, i, 0, 0))
    single = lambda k: pl.BlockSpec((k, N, N), lambda i: (i, 0, 0))
    whole = lambda *d: pl.BlockSpec(d, lambda *_: (0,) * len(d))

    absorbed = pl.pallas_call(
        absorbed_kernel,
        out_shape=shaped(8, NX + 1, 16, N),
        grid=(4,),
        in_specs=[planes(4), single(4), SM, SM],
        out_specs=whole(8, NX + 1, 16, N),
        compiler_params=params(8),
        cost_estimate=cost(10_000_000, 4_000_000),
        name="absorbed",
    )(energy, species, table, fraction)
    gathered = lax.all_to_all(absorbed, "grp", 0, 0, tiled=True)

    own, xa, xb = pl.pallas_call(
        turn_kernel,
        out_shape=(shaped(3, NX, N, N), shaped(3, HE, N, N), shaped(3, HE, N, N)),
        grid=(8,),
        in_specs=[planes(2), single(2)],
        out_specs=(whole(3, NX, N, N), whole(3, HE, N, N), whole(3, HE, N, N)),
        compiler_params=params(14),
        cost_estimate=cost(10_000_000, 8_000_000),
        name="turn",
    )(energy, species)
    xa, xb = exchange(xa, xb, "sx", SX_A, SX_B)
    za, zb = pl.pallas_call(
        functools.partial(corner_kernel, 3, HE),
        out_shape=(shaped(3, NX + 2 * HE, 8, N),) * 2,
        in_specs=[VM] * 3,
        out_specs=(VM, VM),
        compiler_params=params(8),
        cost_estimate=cost(1000, 1_000_000),
        name="corners",
    )(own, xa, xb)
    za, zb = exchange(za, zb, "sz", SZ_A, SZ_B)
    field = shaped(2, PX, ROWS, N)
    scratch = pltpu.VMEM((2, PX, ROWS, N), F32)
    coefs = pl.pallas_call(
        matrix_kernel,
        out_shape=(field,) * 6,
        in_specs=[VM] * 5 + [SM, SM],
        out_specs=(VM,) * 6,
        scratch_shapes=[
            pltpu.VMEM((2, NX + 2 * HE, ROWS, N), F32),
            pltpu.VMEM((NX + 2 * HE, ROWS, N), F32),
            scratch,
            scratch,
        ],
        compiler_params=params(50),
        cost_estimate=cost(100_000_000, 30_000_000),
        name="matrix",
    )(own, xa, xb, za, zb, table, fraction)

    share = pl.BlockSpec((NX, 16, N), lambda i, g: (0, g[0], 0))
    where = lax.axis_index("grp").astype(jnp.int32).reshape(1)
    after = pl.pallas_call(
        temperature_kernel,
        out_shape=shaped(8, NX, 16, N),
        grid_spec=pltpu.PrefetchScalarGridSpec(
            num_scalar_prefetch=1,
            grid=(1,),
            in_specs=[whole(8, NX + 1, 16, N), share, share, share],
            out_specs=whole(8, NX, 16, N),
        ),
        compiler_params=params(8),
        cost_estimate=cost(1_000_000, 3_000_000),
        name="temperature",
    )(where, gathered, kelvin, capacity, species)
    after = lax.all_to_all(after, "grp", 0, 0, tiled=True)
    kelvin_after = jnp.moveaxis(after, 0, 1).reshape(NX, N, N)

    own_t, ta, tb = pl.pallas_call(
        emission_kernel,
        out_shape=(shaped(1, NX, N, N), shaped(1, HT, N, N), shaped(1, HT, N, N)),
        in_specs=[VM],
        out_specs=(VM,) * 3,
        compiler_params=params(8),
        cost_estimate=cost(1_000_000, 3_000_000),
        name="emission",
    )(after)
    ta, tb = exchange(ta, tb, "sx", SX_A, SX_B)
    tza, tzb = pl.pallas_call(
        functools.partial(corner_kernel, 1, HT),
        out_shape=(shaped(1, NX + 2 * HT, 8, N),) * 2,
        in_specs=[VM] * 3,
        out_specs=(VM, VM),
        compiler_params=params(8),
        cost_estimate=cost(1000, 300_000),
        name="corners_t",
    )(own_t, ta, tb)
    tza, tzb = exchange(tza, tzb, "sz", SZ_A, SZ_B)

    v0, v1, v2, mom = pl.pallas_call(
        krylov_kernel,
        out_shape=(field, field, field, shaped(32, 16, N)),
        in_specs=[VM] * 11,
        out_specs=(VM,) * 4,
        scratch_shapes=[pltpu.VMEM((NX + 2 * HT, ROWS, N), F32)],
        compiler_params=params(50),
        cost_estimate=cost(100_000_000, 30_000_000),
        name="krylov",
    )(own_t, ta, tb, tza, tzb, *coefs)
    mom = lax.all_to_all(mom, ("sx", "sz"), 0, 0, tiled=True)
    turned = pl.pallas_call(
        turn_back_kernel,
        out_shape=shaped(3, 2, NX, N, N),
        in_specs=[VM] * 3,
        out_specs=VM,
        compiler_params=params(30),
        cost_estimate=cost(10_000_000, 12_000_000),
        name="turn_back",
    )(v0, v1, v2)
    result = pl.pallas_call(
        update_kernel,
        out_shape=shaped(2, NX, N, N),
        grid=(4,),
        in_specs=[
            whole(32, 16, N),
            planes(4),
            pl.BlockSpec((3, 2, 4, N, N), lambda i: (0, 0, i, 0, 0)),
        ],
        out_specs=planes(4),
        scratch_shapes=[pltpu.VMEM((6, 8, N), F32)],
        compiler_params=params(16),
        cost_estimate=cost(10_000_000, 10_000_000),
        name="update",
    )(mom, energy, turned)
    return result, kelvin_after


def solution(mesh):
    placed = (
        P("grp", "sx", None, "sz"),
        P("sx", None, "sz"),
        P("sx", None, "sz"),
        P("sx", None, "sz"),
        P(None, "grp"),
        P("grp"),
    )
    return jax.shard_map(
        shards,
        mesh=mesh,
        in_specs=placed,
        out_specs=(P("grp", "sx", None, "sz"), P("sx", None, "sz")),
        check_vma=False,
    )
```

```python
import functools

import jax
import jax.numpy as jnp
from jax import lax
from jax.experimental import pallas as pl
from jax.experimental.pallas import tpu as pltpu
from jax.sharding import PartitionSpec as P

DT = 0.5
SHIFT = 6.0
SCALE = 4.0
NX = 16
N = 128
MATS = 8
HE = 5
HT = 3
ROWS = 160
ZO = 16
PX = 24
CHUNKS = ((8, 48), (56, 48), (104, 48))
INNER = ((24, 48), (72, 48), (120, 16))
OUTER = ((8, 16), (136, 16))
OWN = ((16, 48), (64, 48), (112, 32))

SX_A = [(0, 1), (1, 0), (2, 3), (3, 2)]
SX_B = [(1, 2), (2, 1)]
SZ_A = [(0, 1), (1, 0), (2, 3), (3, 2), (4, 5), (5, 4), (6, 7), (7, 6)]
SZ_B = [(1, 2), (2, 1), (3, 4), (4, 3), (5, 6), (6, 5), (7, 0), (0, 7)]

VM = pl.BlockSpec(memory_space=pltpu.VMEM)
HB = pl.BlockSpec(memory_space=pltpu.HBM)
SM = pl.BlockSpec(memory_space=pltpu.SMEM)
F32 = jnp.float32


def shaped(*dims):
    return jax.ShapeDtypeStruct(dims, F32)


def in_vmem(value):
    return pltpu.with_memory_space_constraint(value, pltpu.VMEM)


def in_hbm(value):
    return pltpu.with_memory_space_constraint(value, pltpu.HBM)


def params(mib):
    return pltpu.CompilerParams(vmem_limit_bytes=mib * 1024 * 1024)


def cost(flops, nbytes):
    return pl.CostEstimate(flops=flops, bytes_accessed=nbytes, transcendentals=0)


def pick(species, values):
    b0, b1, b2 = ((species & k) != 0 for k in (1, 2, 4))
    level = [jnp.where(b0, values[2 * k + 1], values[2 * k]) for k in range(4)]
    level = [jnp.where(b1, level[1], level[0]), jnp.where(b1, level[3], level[2])]
    return jnp.where(b2, level[1], level[0])


def absorbed_kernel(e_ref, sp_ref, tab_ref, w_ref, out_ref):
    tabs = [[tab_ref[g, m] for m in range(MATS)] for g in range(2)]
    for k in range(2):
        rows = slice(k * 16, k * 16 + 16)
        for m in range(MATS):
            share = tabs[0][m] * w_ref[0] + tabs[1][m] * w_ref[1]
            out_ref[k, NX, m : m + 1, :] = jnp.full((1, N), share, F32)
        out_ref[k, NX, 8:16, :] = jnp.zeros((8, N), F32)
        for x in range(NX):
            species = sp_ref[x, rows, :]
            out_ref[k, x] = pick(species, tabs[0]) * e_ref[0, x, rows, :] + pick(species, tabs[1]) * e_ref[1, x, rows, :]


def pack_kernel(e_ref, sp_ref, a_ref, b_ref, e_buf, sp_buf, sem):
    even = lax.rem(lax.axis_index("sx"), 2) == 0

    def part(k, first):
        copies = [pltpu.make_async_copy(e_ref.at[g, pl.ds(first, HE)], e_buf.at[k, g], sem.at[k, g]) for g in range(2)]
        copies.append(pltpu.make_async_copy(sp_ref.at[pl.ds(first, HE)], sp_buf.at[k], sem.at[k, 2]))
        return copies

    both = [part(0, jnp.where(even, NX - HE, 0)), part(1, jnp.where(even, 0, NX - HE))]
    for copies in both:
        for copy in copies:
            copy.start()
    for k, out_ref in enumerate((a_ref, b_ref)):
        for copy in both[k]:
            copy.wait()
        for j in range(HE):
            for g in range(2):
                out_ref[g, j] = e_buf[k, g, j].T
            out_ref[2, j] = sp_buf[k, j].astype(F32).T


def turn_kernel(e_ref, sp_ref, out_ref):
    for x in range(4):
        for g in range(2):
            out_ref[g, x] = e_ref[g, x].T
        out_ref[2, x] = sp_ref[x].astype(F32).T


def side_kernel(own_ref, xa_ref, xb_ref, za_ref, zb_ref, sem):
    rows_a, rows_b = slice(0, 8), slice(N - 8, N)

    def send(low, high, first, last):
        copies = []
        for k, (out, rows) in enumerate(((first, rows_a), (last, rows_b))):
            for j, (ref, at, count) in enumerate(((low, 0, HE), (own_ref, HE, NX), (high, HE + NX, HE))):
                copies.append(pltpu.make_async_copy(ref.at[:, :, rows, :], out.at[:, at : at + count], sem.at[k, j]))
        for copy in copies:
            copy.start()
        for copy in copies:
            copy.wait()

    x_even = lax.rem(lax.axis_index("sx"), 2) == 0
    z_even = lax.rem(lax.axis_index("sz"), 2) == 0
    for x_is in (True, False):
        for z_is in (True, False):
            low, high = (xb_ref, xa_ref) if x_is else (xa_ref, xb_ref)
            first, last = (zb_ref, za_ref) if z_is else (za_ref, zb_ref)
            pl.when(jnp.logical_and(x_even == x_is, z_even == z_is))(
                functools.partial(send, low, high, first, last)
            )


def edge_rows(get, depth, a_ref, b_ref):
    even = lax.rem(lax.axis_index("sz"), 2) == 0
    to_a = pl.multiple_of(jnp.where(even, N - 8, 0), 8)
    to_b = pl.multiple_of(jnp.where(even, 0, N - 8), 8)
    for x in range(depth):
        a_ref[x] = get(x, to_a)
        b_ref[x] = get(x, to_b)


def corner_kernel(c_count, halo, own_ref, xa_ref, xb_ref, a_ref, b_ref):
    even = lax.rem(lax.axis_index("sx"), 2) == 0
    for c in range(c_count):

        def fill(low, high):
            def get(x, row):
                if x < halo:
                    return low[c, x, pl.ds(row, 8), :]
                if x < halo + NX:
                    return own_ref[c, x - halo, pl.ds(row, 8), :]
                return high[c, x - halo - NX, pl.ds(row, 8), :]

            edge_rows(get, NX + 2 * halo, a_ref.at[c], b_ref.at[c])

        pl.when(even)(lambda: fill(xb_ref, xa_ref))
        pl.when(jnp.logical_not(even))(lambda: fill(xa_ref, xb_ref))


def lanes(n):
    return lax.broadcasted_iota(jnp.int32, (n, N), 1)


def height(row, n):
    return lax.broadcasted_iota(jnp.int32, (n, N), 0) + (lax.axis_index("sz") * N + row - ZO)


def limiter_kernel(own_ref, xa_ref, xb_ref, za_ref, zb_ref, tab_ref, e_ref, d_ref, op_ref, spx_ref, sem):
    sx, sz = lax.axis_index("sx"), lax.axis_index("sz")
    tabs = [[tab_ref[g, m] for m in range(MATS)] for g in range(2)]
    below, middle, above = slice(ZO - 8, ZO), slice(ZO, ZO + N), slice(ZO + N, ZO + N + 8)
    x_even = lax.rem(sx, 2) == 0
    z_even = lax.rem(sz, 2) == 0

    def piece(c, ref, source, first, count, rows, k):
        planes = slice(first, first + count)
        target = spx_ref.at[planes, rows, :] if c == 2 else e_ref.at[c, planes, rows, :]
        return pltpu.make_async_copy(ref.at[c, source : source + count], target, sem.at[k, c])

    def start(low, high, x_low, x_high):
        for c in range(3):
            piece(c, x_low, 0, 0, HE, middle, 0).start()
            piece(c, low, 0, 0, NX + 2 * HE, below, 3).start()
            piece(c, high, 0, 0, NX + 2 * HE, above, 4).start()
            piece(c, own_ref, 0, HE, NX // 2, middle, 1).start()
            piece(c, own_ref, NX // 2, HE + NX // 2, NX // 2, middle, 2).start()
            piece(c, x_high, 0, HE + NX, HE, middle, 5).start()

    for x_is in (True, False):
        for z_is in (True, False):
            x_low, x_high = (xb_ref, xa_ref) if x_is else (xa_ref, xb_ref)
            low, high = (zb_ref, za_ref) if z_is else (za_ref, zb_ref)
            pl.when(jnp.logical_and(x_even == x_is, z_even == z_is))(
                functools.partial(start, low, high, x_low, x_high)
            )

    def finish(k, ref, source, first, count, rows):
        for c in range(3):
            piece(c, ref, source, first, count, rows, k).wait()

    finish(0, xa_ref, 0, 0, HE, middle)
    finish(3, za_ref, 0, 0, NX + 2 * HE, below)
    finish(4, za_ref, 0, 0, NX + 2 * HE, above)

    def clear(rows):
        def step(x, carry):
            for g in range(2):
                e_ref[g, x, rows, :] = jnp.zeros((8, N), F32)
            return carry

        lax.fori_loop(0, NX + 2 * HE, step, 0)

    pl.when(sz == 0)(lambda: clear(below))
    pl.when(sz == 7)(lambda: clear(above))
    finish(1, own_ref, 0, HE, NX // 2, middle)

    def coefficients(p, carry):
        pl.when(p == HE + NX // 2 - 2)(
            lambda: finish(2, own_ref, NX // 2, HE + NX // 2, NX // 2, middle)
        )
        pl.when(p == HE + NX - 2)(lambda: finish(5, xa_ref, 0, HE + NX, HE, middle))
        gx = sx * NX + p - 4
        x_in = jnp.logical_and(gx >= 0, gx < 4 * NX).astype(jnp.int32)
        for row, n in CHUNKS:
            gz = height(row, n)
            inside = jnp.logical_and(gz >= 0, gz < 8 * N * x_in)
            lane = lanes(n)
            rows = slice(row, row + n)
            species = spx_ref[p + 1, rows, :].astype(jnp.int32)
            for g in range(2):
                opacity = pick(species, tabs[g])
                center = e_ref[g, p + 1, rows, :]
                dx = e_ref[g, p + 2, rows, :] - e_ref[g, p, rows, :]
                dz = e_ref[g, p + 1, row + 1 : row + 1 + n, :] - e_ref[g, p + 1, row - 1 : row - 1 + n, :]
                above = jnp.where(lane == N - 1, 0.0, pltpu.roll(center, N - 1, 1))
                below = jnp.where(lane == 0, 0.0, pltpu.roll(center, 1, 1))
                dy = above - below
                square = 0.25 * (dx * dx + dy * dy + dz * dz)
                slope = jnp.sqrt(square)
                m = opacity * center
                upper = m * (2.0 * m + slope)
                lower = opacity * (m * (6.0 * m + 3.0 * slope) + square)
                d_ref[g, p, rows, :] = jnp.where(inside, upper / lower, 0.0)
                op_ref[g, p, rows, :] = opacity
        return carry

    lax.fori_loop(0, PX, coefficients, 0)


def operator_kernel(e_ref, d_ref, op_ref, w_ref, dg_ref, kx_ref, ky_ref, kz_ref, q_ref, ow_ref):
    sx = lax.axis_index("sx")
    inv = 1.0 / SCALE

    def operator(p, carry):
        gx = sx * NX + p - 4
        x_in = jnp.logical_and(gx >= 0, gx < 4 * NX).astype(jnp.int32)
        x_face = jnp.where(jnp.logical_and(gx >= 0, gx + 1 < 4 * NX), 0.5, 0.0)
        for row, n in CHUNKS:
            gz = height(row, n)
            inside = jnp.logical_and(gz >= 0, gz < 8 * N * x_in)
            z_face = jnp.where(jnp.logical_and(gz >= 0, gz + 1 < 8 * N), 0.5, 0.0)
            lane = lanes(n)
            rows = slice(row, row + n)
            up = slice(row + 1, row + 1 + n)
            down = slice(row - 1, row - 1 + n)
            for g in range(2):
                d = d_ref[g, p, rows, :]
                dxp, dxm = d_ref[g, p + 1, rows, :], d_ref[g, p - 1, rows, :]
                dzp, dzm = d_ref[g, p, up, :], d_ref[g, p, down, :]
                dyp = jnp.where(lane == N - 1, 0.0, pltpu.roll(d, N - 1, 1))
                dym = jnp.where(lane == 0, 0.0, pltpu.roll(d, 1, 1))
                opacity = op_ref[g, p, rows, :]
                sxp, sxm, szp, szm, syp, sym = (d + o for o in (dxp, dxm, dzp, dzm, dyp, dym))
                total = 0.5 * (((sxp + sxm) + (szp + szm)) + (syp + sym))
                diag = (1.0 / DT + opacity) + total
                center = e_ref[g, p + 1, rows, :]
                moved = (
                    (sxp * e_ref[g, p + 2, rows, :] + sxm * e_ref[g, p, rows, :])
                    + (szp * e_ref[g, p + 1, up, :] + szm * e_ref[g, p + 1, down, :])
                    + jnp.where(lane == N - 1, 0.0, syp * pltpu.roll(center, N - 1, 1))
                    + jnp.where(lane == 0, 0.0, sym * pltpu.roll(center, 1, 1))
                )
                q_ref[g, p, rows, :] = jnp.where(inside, (1.0 / DT - diag) * center + 0.5 * moved, 0.0)
                ow_ref[g, p, rows, :] = jnp.where(inside, opacity * w_ref[g], 0.0)
                dg_ref[g, p, rows, :] = jnp.where(inside, (diag - SHIFT) * inv, 0.0)
                kx_ref[g, p, rows, :] = sxp * (x_face * inv)
                kz_ref[g, p, rows, :] = szp * (z_face * inv)
                ky_ref[g, p, rows, :] = jnp.where(lane == N - 1, 0.0, syp * (0.5 * inv))
        return carry

    lax.fori_loop(1, PX - 1, operator, 0)


def temperature_kernel(g_ref, r_ref, t_ref, cap_ref, sp_ref, out_ref):
    shares = r_ref[0, NX, 0:8, :]
    for k in range(1, 8):
        shares = shares + r_ref[k, NX, 0:8, :]
    values = [jnp.broadcast_to(shares[m : m + 1, :], (16, N)) for m in range(MATS)]
    for x in range(NX):
        absorbed = r_ref[0, x]
        for k in range(1, 8):
            absorbed = absorbed + r_ref[k, x]
        t = t_ref[x]
        weight = pick(sp_ref[x], values)
        cube = t * t * t
        gain = absorbed - weight * (cube * t)
        slope = 4.0 * weight * cube
        after = t + DT * gain / (cap_ref[x] + DT * slope)
        for k in range(8):
            out_ref[k, x] = after


def emission_kernel(t_ref, out_ref, a_ref, b_ref, after_ref):
    for x in range(NX):
        t = t_ref[:, x].reshape(N, N)
        after_ref[x] = t
        square = t * t
        out_ref[0, x] = (square * square).T
    even = lax.rem(lax.axis_index("sx"), 2) == 0
    to_a = jnp.where(even, NX - HT, 0)
    to_b = jnp.where(even, 0, NX - HT)
    for j in range(HT):
        a_ref[0, j] = out_ref[0, to_a + j]
        b_ref[0, j] = out_ref[0, to_b + j]


def applied(v_ref, dg_ref, kx_ref, ky_ref, kz_ref, g, p, row, n):
    rows = slice(row, row + n)
    up = slice(row + 1, row + 1 + n)
    down = slice(row - 1, row - 1 + n)
    c = v_ref[g, p, rows, :]
    ky = ky_ref[g, p, rows, :]
    total = dg_ref[g, p, rows, :] * c
    total = total - kx_ref[g, p, rows, :] * v_ref[g, p + 1, rows, :]
    total = total - kx_ref[g, p - 1, rows, :] * v_ref[g, p - 1, rows, :]
    total = total - kz_ref[g, p, rows, :] * v_ref[g, p, up, :]
    total = total - kz_ref[g, p, down, :] * v_ref[g, p, down, :]
    total = total - ky * pltpu.roll(c, N - 1, 1)
    return total - pltpu.roll(ky * c, 1, 1)


def inner_kernel(
    own_ref, xa_ref, xb_ref, dg_ref, kx_ref, ky_ref, kz_ref, q_ref, ow_ref, v0_ref, v1_ref
):
    def first(plane, ref, count):
        def step(j, carry):
            p = plane + j
            for row, n in OWN:
                rows = slice(row, row + n)
                t = ref[0, j, row - ZO : row - ZO + n, :]
                for g in range(2):
                    v0_ref[g, p, rows, :] = q_ref[g, p, rows, :] + ow_ref[g, p, rows, :] * t
            return carry

        lax.fori_loop(0, count, step, 0)

    even = lax.rem(lax.axis_index("sx"), 2) == 0

    def sides(low, high):
        first(4 - HT, low, HT)
        first(4 + NX, high, HT)

    pl.when(even)(lambda: sides(xb_ref, xa_ref))
    pl.when(jnp.logical_not(even))(lambda: sides(xa_ref, xb_ref))
    first(4, own_ref, NX)

    def second(p, carry):
        for g in range(2):
            for row, n in INNER:
                v1_ref[g, p, row : row + n, :] = applied(v0_ref, dg_ref, kx_ref, ky_ref, kz_ref, g, p, row, n)
        return carry

    lax.fori_loop(2, PX - 2, second, 0)


def krylov_kernel(
    za_ref, zb_ref, dg_ref, kx_ref, ky_ref, kz_ref, v0_in, v1_in, ow_ref,
    v0_ref, v1_ref, v2_ref, mom_ref,
):
    apply = functools.partial(applied, dg_ref=dg_ref, kx_ref=kx_ref, ky_ref=ky_ref, kz_ref=kz_ref)

    def edges(low, high):
        def step(p, carry):
            for g in range(2):
                for row, t in ((ZO - 4, low[0, p - 1, 4:8, :]), (ZO + N, high[0, p - 1, 0:4, :])):
                    rows = slice(row, row + 4)
                    v0_ref[g, p, rows, :] = v0_ref[g, p, rows, :] + ow_ref[g, p, rows, :] * t
            return carry

        lax.fori_loop(1, PX - 1, step, 0)

    z_even = lax.rem(lax.axis_index("sz"), 2) == 0
    pl.when(z_even)(lambda: edges(zb_ref, za_ref))
    pl.when(jnp.logical_not(z_even))(lambda: edges(za_ref, zb_ref))

    for source, target, start, chunks in ((v0_ref, v1_ref, 2, OUTER), (v1_ref, v2_ref, 3, CHUNKS)):

        def step(p, carry, source=source, target=target, chunks=chunks):
            for g in range(2):
                for row, n in chunks:
                    target[g, p, row : row + n, :] = apply(source, g=g, p=p, row=row, n=n)
            return carry

        lax.fori_loop(start, PX - start, step, 0)

    def fold(value):
        return jnp.sum(value.reshape(-1, 8, N), axis=0)

    for g in range(2):

        def last(p, sums, g=g):
            sums = list(sums)
            for row, n in OWN:
                rows = slice(row, row + n)
                a, b, c = v0_ref[g, p, rows, :], v1_ref[g, p, rows, :], v2_ref[g, p, rows, :]
                d = apply(v2_ref, g=g, p=p, row=row, n=n)
                for k, (l, r) in enumerate(((a, a), (a, b), (b, b), (b, c), (c, c), (c, d))):
                    sums[k] = sums[k] + fold(l * r)
            return tuple(sums)

        sums = lax.fori_loop(4, 4 + NX, last, (jnp.zeros((8, N), F32),) * 6)
        for k in range(6):
            line = jnp.sum(sums[k], axis=0, keepdims=True)
            for peer in range(mom_ref.shape[0]):
                mom_ref[peer, g * 8 + k : g * 8 + k + 1, :] = line
        for peer in range(mom_ref.shape[0]):
            mom_ref[peer, g * 8 + 6 : g * 8 + 8, :] = jnp.zeros((2, N), F32)


def update_kernel(mom_ref, e_ref, v0_ref, v1_ref, v2_ref, out_ref, c_ref):
    @pl.when(pl.program_id(0) == 0)
    def _():
        total = mom_ref[0]
        for k in range(1, mom_ref.shape[0]):
            total = total + mom_ref[k]
        total = jnp.sum(total, axis=1, keepdims=True)
        for g in range(2):
            n = [total[g * 8 + k : g * 8 + k + 1, :] for k in range(6)]
            m = [SHIFT * n[k] + SCALE * n[k + 1] for k in range(5)]
            l1 = m[1] / m[0]
            l2 = m[2] / m[0]
            p1 = m[2] - l1 * m[1]
            u = m[3] - l1 * m[2]
            r1 = n[1] - l1 * n[0]
            ok1 = p1 > 1e-6 * m[2]
            s1 = jnp.where(ok1, u / p1, 0.0)
            p2 = m[4] - l2 * m[2] - s1 * u
            r2 = n[2] - l2 * n[0] - s1 * r1
            ok2 = jnp.logical_and(ok1, p2 > 1e-6 * m[4])
            c2 = jnp.where(ok2, r2 / p2, 0.0)
            c1 = jnp.where(ok1, (r1 - u * c2) / p1, 0.0)
            c0 = (n[0] - m[1] * c1 - m[2] * c2) / m[0]
            for k, c in enumerate((c0, c1, c2)):
                c_ref[g * 3 + k] = jnp.broadcast_to(c, (8, N))

    rows = slice(ZO, ZO + N)
    for x in range(4):
        p = pl.program_id(0) * 4 + (x + 4)
        for g in range(2):
            total = v0_ref[g, p, rows, :] * c_ref[g * 3, 0:1, :]
            total = total + v1_ref[g, p, rows, :] * c_ref[g * 3 + 1, 0:1, :]
            total = total + v2_ref[g, p, rows, :] * c_ref[g * 3 + 2, 0:1, :]
            out_ref[g, x] = e_ref[g, x] + total.T


def exchange(a, b, axis, pair_a, pair_b):
    return lax.ppermute(a, axis, pair_a), lax.ppermute(b, axis, pair_b)


def shards(energy, kelvin, capacity, species, table, fraction):
    table = table.T
    planes = lambda k: pl.BlockSpec((2, k, N, N), lambda i: (0, i, 0, 0))
    single = lambda k: pl.BlockSpec((k, N, N), lambda i: (i, 0, 0))
    whole = lambda *d: pl.BlockSpec(d, lambda *_: (0,) * len(d))

    absorbed = pl.pallas_call(
        absorbed_kernel,
        out_shape=shaped(8, NX + 1, 16, N),
        grid=(4,),
        in_specs=[
            pl.BlockSpec((2, NX, 32, N), lambda i: (0, 0, i, 0)),
            pl.BlockSpec((NX, 32, N), lambda i: (0, i, 0)),
            SM,
            SM,
        ],
        out_specs=pl.BlockSpec((2, NX + 1, 16, N), lambda i: (i, 0, 0, 0)),
        compiler_params=params(60),
        cost_estimate=cost(10_000_000, 4_000_000),
        name="absorbed",
    )(energy, species, table, fraction)
    gathered = lax.all_to_all(absorbed, "grp", 0, 0, tiled=True)

    field = pltpu.VMEM((2, PX, ROWS, N), F32)
    wide = pltpu.VMEM((2, NX + 2 * HE, ROWS, N), F32)
    xa, xb = pl.pallas_call(
        pack_kernel,
        out_shape=(pltpu.HBM((3, HE, N, N), F32),) * 2,
        in_specs=[HB, HB],
        out_specs=(VM, VM),
        scratch_shapes=[
            pltpu.VMEM((2, 2, HE, N, N), F32),
            pltpu.VMEM((2, HE, N, N), jnp.int32),
            pltpu.SemaphoreType.DMA((2, 3)),
        ],
        compiler_params=params(6),
        cost_estimate=cost(1_000_000, 4_000_000),
        name="pack",
    )(in_hbm(energy), in_hbm(species))
    xa, xb = map(in_vmem, exchange(xa, xb, "sx", SX_A, SX_B))
    own = pl.pallas_call(
        turn_kernel,
        out_shape=pltpu.HBM((3, NX, N, N), F32),
        grid=(4,),
        in_specs=[planes(4), single(4)],
        out_specs=pl.BlockSpec((3, 4, N, N), lambda i: (0, i, 0, 0)),
        compiler_params=params(8),
        cost_estimate=cost(10_000_000, 8_000_000),
        name="turn",
    )(in_hbm(energy), in_hbm(species))
    gathered, own = lax.optimization_barrier((gathered, own))
    za, zb = pl.pallas_call(
        side_kernel,
        out_shape=(pltpu.HBM((3, NX + 2 * HE, 8, N), F32),) * 2,
        in_specs=[HB, VM, VM],
        out_specs=(VM,) * 2,
        scratch_shapes=[pltpu.SemaphoreType.DMA((2, 3))],
        compiler_params=params(2),
        cost_estimate=cost(1000, 1_000_000),
        name="sides",
    )(in_hbm(own), xa, xb)
    za, zb = map(in_vmem, exchange(za, zb, "sz", SZ_A, SZ_B))
    ext, diffusion, opacity = pl.pallas_call(
        limiter_kernel,
        out_shape=(wide, field, field),
        in_specs=[HB] + [VM] * 4 + [SM],
        out_specs=(VM,) * 3,
        scratch_shapes=[
            pltpu.VMEM((NX + 2 * HE, ROWS, N), F32),
            pltpu.SemaphoreType.DMA((6, 3)),
        ],
        compiler_params=params(5),
        cost_estimate=cost(100_000_000, 15_000_000),
        name="limiter",
    )(in_hbm(own), xa, xb, za, zb, table)
    share = pl.BlockSpec((NX, 16, N), lambda i, g: (0, g[0], 0))
    where = lax.axis_index("grp").astype(jnp.int32).reshape(1)
    after = pl.pallas_call(
        temperature_kernel,
        out_shape=pltpu.HBM((8, NX, 16, N), F32),
        grid_spec=pltpu.PrefetchScalarGridSpec(
            num_scalar_prefetch=1,
            grid=(1,),
            in_specs=[VM, share, share, share],
            out_specs=whole(8, NX, 16, N),
        ),
        compiler_params=params(8),
        cost_estimate=cost(1_000_000, 3_000_000),
        name="temperature",
    )(where, gathered, in_hbm(kelvin), in_hbm(capacity), in_hbm(species))
    after = lax.all_to_all(after, "grp", 0, 0, tiled=True)

    own_t, ta, tb, kelvin_after = pl.pallas_call(
        emission_kernel,
        out_shape=(shaped(1, NX, N, N), shaped(1, HT, N, N), shaped(1, HT, N, N), shaped(NX, N, N)),
        in_specs=[VM],
        out_specs=(VM,) * 4,
        compiler_params=params(6),
        cost_estimate=cost(1_000_000, 3_000_000),
        name="emission",
    )(after)
    ta, tb = exchange(ta, tb, "sx", SX_A, SX_B)
    own_t, diffusion = lax.optimization_barrier((own_t, diffusion))
    tza, tzb = pl.pallas_call(
        functools.partial(corner_kernel, 1, HT),
        out_shape=(shaped(1, NX + 2 * HT, 8, N),) * 2,
        in_specs=[VM] * 3,
        out_specs=(VM, VM),
        compiler_params=params(9),
        cost_estimate=cost(1000, 300_000),
        name="corners_t",
    )(own_t, ta, tb)
    tza, tzb = exchange(tza, tzb, "sz", SZ_A, SZ_B)

    *coefs, q, emit = pl.pallas_call(
        operator_kernel,
        out_shape=(field,) * 6,
        in_specs=[VM] * 3 + [SM],
        out_specs=(VM,) * 6,
        input_output_aliases={2: 5},
        compiler_params=params(4),
        cost_estimate=cost(100_000_000, 15_000_000),
        name="operator",
    )(in_vmem(ext), in_vmem(diffusion), in_vmem(opacity), fraction)

    v0, v1 = pl.pallas_call(
        inner_kernel,
        out_shape=(field, field),
        in_specs=[VM] * 9,
        out_specs=(VM,) * 2,
        input_output_aliases={7: 0},
        compiler_params=params(4),
        cost_estimate=cost(50_000_000, 10_000_000),
        name="inner",
    )(own_t, ta, tb, *map(in_vmem, (*coefs, q, emit)))
    v0, v1, v2, mom = pl.pallas_call(
        krylov_kernel,
        out_shape=(field, field, field, pltpu.HBM((32, 16, N), F32)),
        in_specs=[VM] * 9,
        out_specs=(VM,) * 4,
        input_output_aliases={6: 0, 7: 1, 8: 2},
        compiler_params=params(4),
        cost_estimate=cost(100_000_000, 30_000_000),
        name="krylov",
    )(tza, tzb, *map(in_vmem, (*coefs, v0, v1, emit)))
    mom = lax.all_to_all(mom, ("sx", "sz"), 0, 0, tiled=True)
    result = pl.pallas_call(
        update_kernel,
        out_shape=shaped(2, NX, N, N),
        grid=(4,),
        in_specs=[
            whole(32, 16, N),
            planes(4),
            VM,
            VM,
            VM,
        ],
        out_specs=planes(4),
        scratch_shapes=[pltpu.VMEM((6, 8, N), F32)],
        compiler_params=params(16),
        cost_estimate=cost(10_000_000, 10_000_000),
        name="update",
    )(mom, energy, in_vmem(v0), in_vmem(v1), in_vmem(v2))
    return result, kelvin_after


def solution(mesh):
    placed = (
        P("grp", "sx", None, "sz"),
        P("sx", None, "sz"),
        P("sx", None, "sz"),
        P("sx", None, "sz"),
        P(None, "grp"),
        P("grp"),
    )
    return jax.shard_map(
        shards,
        mesh=mesh,
        in_specs=placed,
        out_specs=(P("grp", "sx", None, "sz"), P("sx", None, "sz")),
        check_vma=False,
    )
```
